32 devices in a mesh: grp: 2 (over x), clu: 2 (over core), slab: 8 (over z, y).
Axes of the slice: x: 2, y: 2, z: 4, core: 2. Of those that a mesh axis runs over, the one named last changes fastest.
Arguments:
- candidates: bfloat16 [768, 1024], P(('grp', 'clu', 'slab')), parts along dimension 0, may hold values from -6 to 6
- cluster_ids: int32 [768, 1], P(('grp', 'clu', 'slab')), parts along dimension 0, may hold values from 0 to 1; in each aligned block of 24 rows (0 to 23, 24 to 47, ...) at most 16 rows name the same one
- pool: bfloat16 [65536, 1024], P(('grp', 'clu', 'slab')), parts along dimension 0, may hold values from -6 to 6
- pool_valid: int32 [65536], P(('grp', 'clu', 'slab')), parts along dimension 0, may hold values from 0 to 1, as said below
Outputs:
- drift: float32 [768, 1024], P(('grp', 'clu', 'slab')), parts along dimension 0
- density: float32 [768], P(('grp', 'clu', 'slab')), parts along dimension 0
The draws below stay inside these ranges and needn't reach their ends.
There are 2 independent parts, one for each index of `grp`. The reference program is written for one: setup_inputs(seed, part) draws one part's arguments, and reference() takes and returns one part's arrays. A program takes and returns all parts, laid end to end along the dimension named above; each array names one. Nothing has to cross between parts.
Inputs may be any that keep to these rules, and one draw needn't show every extreme that they name: `cluster_ids`: among the rows of one device, at most 16 candidates name one cluster, and in some device exactly 16 do. `pool_valid`: the first row of every device's pool block is live.
All inputs are finite; a program needn't handle non-finite values.
Results may differ from the reference program's by a relative error of at most 0.0091.
Values may be sent and summed in bfloat16 or wider, within the bound.
A program may use at most 64 MiB of HBM per device.

```python
import math
import jax
import jax.numpy as jnp
import numpy as np
from jax import lax

D = 1024
B_DEV = 24
POOL_DEV = 2048
CAP = 16
CAND = 384
CLU_ROWS = 16384
POOL_ROWS = 32768
N_CLU = 2


def draw_pool_valid(key, part):
    rows = jnp.arange(POOL_ROWS, dtype=jnp.int32)
    inside = rows % CLU_ROWS
    limit = 250 + 700 * inside // CLU_ROWS
    roll = jax.random.randint(key, (POOL_ROWS,), 0, 1000, dtype=jnp.int32)
    live = (roll < limit) | (rows % POOL_DEV == 0)
    return jnp.where(live, 1, 0).astype(jnp.int32)


def steps_of(key, extent, shards, least, largest):
    def one(position, shards_of):
        heights = jax.random.uniform(jax.random.fold_in(jax.random.fold_in(key, 6), position), (shards_of,), jnp.float32, least / len(shards), largest / len(shards))
        return jnp.repeat(jnp.exp(heights), extent[position] // shards_of).reshape((-1,) + (1,) * (len(extent) - position - 1))

    factor_of = one(*shards[0])
    for cut in shards[1:]:
        factor_of = factor_of * one(*cut)
    return factor_of


def assign_block(rng, own, number, rows, count, top, most, slope):
    order = jax.random.permutation(rng, count)
    heavy_load, ordinary = shares(count, rows * top, most, slope, True), shares(count, rows * top, most, slope, False)
    places = jnp.arange(count)

    def named(lengths, rotation):
        used = int((lengths > 0).sum())
        fixed = max(1, used // 4)
        moved = fixed + (places - fixed + rotation * (used - fixed)) % max(1, count - fixed)
        return jnp.zeros((count,), jnp.int32).at[order[jnp.where(places < fixed, places, moved)]].set(jnp.asarray(lengths, jnp.int32))

    lengths = jnp.where(number % 4 == 0, named(heavy_load, number // 4), named(ordinary, number - number // 4 - 1))
    mixed = jax.random.permutation(jax.random.fold_in(own, 3), count)
    source_of, taker = mixed[0:count // 2 * 2:2], mixed[1:count // 2 * 2:2]
    room = jnp.minimum(lengths[source_of] - 1, most - lengths[taker]) // 2
    room = jnp.where((source_of == order[0]) | (taker == order[0]) | (lengths[taker] == 0), 0, jnp.maximum(room, 0))
    moved = jax.random.randint(jax.random.fold_in(own, 4), (count // 2,), 0, 1 << 20) % (room + 1)
    lengths = lengths.at[source_of].add(-moved).at[taker].add(moved)
    items = jnp.searchsorted(jnp.cumsum(lengths), jnp.arange(rows * top), side="right").astype(jnp.int32)
    table = items.reshape(top, rows).T
    table = table[jax.random.permutation(jax.random.fold_in(own, 1), rows)]
    rotation = jax.random.randint(jax.random.fold_in(own, 2), (rows, 1), 0, top)
    return jnp.take_along_axis(table, (jnp.arange(top)[None, :] + rotation) % top, axis=1)


def shares(count, total, most, lean, full):
    loads = [(1 << 20) // math.isqrt(grade ** lean) + 1 for grade in range(1, count + 1)]
    largest = most if full else min(most, max(-(-total // count), total * loads[0] // sum(loads)))
    least = 1 if total - largest >= count - 1 else 0
    counts, surplus = [largest] + [least] * (count - 1), total - largest - least * (count - 1)
    while surplus > 0:
        free = [i for i in range(1, count) if counts[i] < largest] or [i for i in range(1, count) if counts[i] < most]
        whole, left = sum([loads[i] for i in free]), surplus
        for i in free:
            addition = min(most - counts[i], max(1, left * loads[i] // whole), surplus)
            counts[i] = counts[i] + addition
            surplus = surplus - addition
    return np.array(counts)


def normal_values(key, dims, spread, most, cuts=(), kind=jnp.bfloat16):
    entries = jax.random.normal(key, dims, jnp.float32) * spread
    if len(cuts) > 0:
        entries = steps_of(key, dims, cuts, -0.22, 0.18) * entries
    return jnp.clip(entries, min=-most, max=most).astype(kind)


def setup_inputs(seed: int = 0, part: int = 0) -> dict:
    keys = jax.random.split(jax.random.key(seed), 5)
    part_keys = jax.random.split(jax.random.fold_in(keys[4], part), 5)
    candidates = normal_values(part_keys[0], (CAND, D), 1.0, 6.0, ((0, 16),))
    cluster_ids_keys = jax.random.split(jax.random.fold_in(part_keys[1], 1), CAND // B_DEV)
    cluster_ids_turns = jax.random.permutation(jax.random.fold_in(part_keys[1], 3), CAND // B_DEV)
    cluster_ids = jax.vmap(lambda own, number: assign_block(jax.random.fold_in(part_keys[1], 2), own, number, B_DEV, N_CLU, 1, CAP, 2))(cluster_ids_keys, cluster_ids_turns).reshape((CAND, 1))
    pool = normal_values(part_keys[2], (POOL_ROWS, D), 1.0, 6.0, ((0, 16),))
    pool_valid = draw_pool_valid(jax.random.fold_in(jax.random.fold_in(keys[4], part), 71), part)
    return dict(candidates=candidates, cluster_ids=cluster_ids, pool=pool, pool_valid=pool_valid)


def rms_rows(data):
    wide = data.astype(jnp.float32)
    factor = lax.rsqrt(lax.optimization_barrier(jnp.mean(wide * wide, axis=-1, keepdims=True)) + 1e-06)
    return (wide * factor).astype(jnp.bfloat16)

def finish(summed, total, width, clu_rows):
    drift = 0.5 * math.sqrt(width) * summed / total[:, None]
    return (drift, total / clu_rows)

def reference(candidates, cluster_ids, pool, pool_valid):
    width = candidates.shape[1]
    sharp = 2.0 * math.sqrt(width)
    unit_rows = rms_rows(candidates)
    pool_unit = rms_rows(pool)
    valid_f = pool_valid.astype(jnp.float32)
    labels = cluster_ids[:, 0]
    drift = jnp.zeros((CAND, width), jnp.float32)
    density = jnp.zeros((CAND,), jnp.float32)
    for group in range(N_CLU):
        part_pool = pool_unit[group * CLU_ROWS:(group + 1) * CLU_ROWS].astype(jnp.float32)
        part_valid = valid_f[group * CLU_ROWS:(group + 1) * CLU_ROWS]

        def one_block(rows):
            score = jnp.dot(rows.astype(jnp.float32), part_pool.T, precision=lax.Precision.HIGHEST)
            weight = part_valid[None, :] * jnp.exp(sharp * (score / width))
            total = lax.optimization_barrier(jnp.sum(weight, axis=1))
            low = weight.astype(jnp.bfloat16).astype(jnp.float32)
            summed = jnp.dot(low, part_pool, precision=lax.Precision.HIGHEST)
            return (summed, total)
        summed, total = lax.map(one_block, unit_rows.reshape(-1, B_DEV, width))
        summed = summed.reshape(CAND, width)
        total = total.reshape(CAND)
        part_drift, part_density = finish(summed, total, width, float(CLU_ROWS))
        chosen = labels == group
        drift = jnp.where(chosen[:, None], part_drift, drift)
        density = jnp.where(chosen, part_density, density)
    return (drift, density)
```

```python
import functools
import math

import jax
import jax.numpy as jnp
from jax import lax
from jax.experimental import pallas as pl
from jax.experimental.pallas import tpu as pltpu
from jax.sharding import PartitionSpec as P

CAP = 16
CHUNKS = 2
LAG = 1
MESH = pl.DeviceIdType.MESH


def rms_rows(data):
    wide = data.astype(jnp.float32)
    factor = lax.rsqrt(jnp.mean(wide * wide, axis=-1, keepdims=True) + 1e-06)
    return (wide * factor).astype(jnp.bfloat16)


def kernel(dims, cand_hbm, ids_hbm, valid_hbm, pool_ref, drift_ref, dens_ref,
           cand_ref, ids_ref, valid_ref, unit, outgoing, every, low,
           ysend, yrecv, own, zsend, zrecv, mysend, myrecv, mown, mzsend, mzrecv,
           in_sem, pool_sem, s1, r1, sy, ry, sz, rz):
    groups, nz, ny, tiles, chunks, clu_rows = dims
    count, width = cand_ref.shape
    pool_rows = pool_ref.shape[0]
    rows_tile = pool_rows // tiles
    chunk = width // chunks
    sharp = 2.0 * math.sqrt(width)
    c = lax.axis_index("clu")
    slab = lax.axis_index("slab")
    z, y = lax.div(slab, ny), lax.rem(slab, ny)

    def device(dc, dy, dz):
        pz, py = lax.rem(z + dz, nz), lax.rem(y + dy, ny)
        return {"clu": lax.rem(c + dc, groups), "slab": pz * ny + py}

    hops = sorted(range(1, nz), key=lambda d: (min(d, nz - d), d))
    near = [(dc, 0, dz) for dz in hops for dc in range(groups)]
    side = [(dc, 1, 0) for dc in range(groups)] if ny == 2 else []
    twin = [(dc, 0, 0) for dc in range(1, groups)]
    far = [(dc, 1, dz) for dz in hops for dc in range(groups)] if ny == 2 else []
    direct = near + side + twin

    def index(offset):
        return (offset[0] * ny + offset[1]) * nz + offset[2]

    inputs = []
    for i, (src, dst) in enumerate(
        [(cand_hbm, cand_ref), (ids_hbm, ids_ref), (valid_hbm, valid_ref)]
    ):
        load = pltpu.make_async_copy(src, dst, in_sem.at[i])
        load.start()
        inputs.append(load)
    loads = []
    for t in range(tiles):
        span = pl.ds(t * rows_tile, rows_tile)
        load = pltpu.make_async_copy(pool_ref.at[span], unit.at[span], pool_sem.at[t])
        load.start()
        loads.append(load)

    barrier = pltpu.get_barrier_semaphore()
    for offset in direct:
        pl.semaphore_signal(barrier, inc=1, device_id=device(*offset), device_id_type=MESH)

    inputs[0].wait()
    inputs[1].wait()
    ids = ids_ref[...]
    member = (
        lax.broadcasted_iota(jnp.int32, (groups, count), 0) == ids
    ).astype(jnp.float32)
    upper = (
        lax.broadcasted_iota(jnp.int32, (count, count), 0)
        <= lax.broadcasted_iota(jnp.int32, (count, count), 1)
    ).astype(jnp.float32)
    ranks = jnp.dot(member, upper, preferred_element_type=jnp.float32)
    place = jnp.sum(member * ranks, axis=0, keepdims=True) - 1.0
    slot = ids * CAP + place.astype(jnp.int32)
    picked = lax.broadcasted_iota(jnp.int32, (groups * CAP, count), 0) == slot
    picker = picked.astype(jnp.float32)
    sent = jnp.dot(
        picker.astype(jnp.bfloat16), rms_rows(cand_ref[...]), preferred_element_type=jnp.float32
    ).astype(jnp.bfloat16)
    for g in range(groups):
        outgoing[g] = sent[g * CAP : (g + 1) * CAP]
    every[0, z, c] = outgoing[c]

    pl.semaphore_wait(barrier, len(direct))

    copies = {}
    for offset in direct:
        copy = pltpu.make_async_remote_copy(
            src_ref=outgoing.at[lax.rem(c + offset[0], groups)],
            dst_ref=every.at[offset[1], z, c],
            send_sem=s1.at[index(offset)],
            recv_sem=r1.at[index(offset)],
            device_id=device(*offset),
            device_id_type=MESH,
        )
        copy.start()
        copies[offset] = copy

    def forward(dc, dz):
        copies[(dc, 0, dz)].wait_recv()
        if ny == 2:
            fc, fz = lax.rem(c + groups - dc, groups), lax.rem(z + nz - dz, nz)
            offset = (dc, 1, dz)
            copy = pltpu.make_async_remote_copy(
                src_ref=every.at[0, fz, fc],
                dst_ref=every.at[1, fz, fc],
                send_sem=s1.at[index(offset)],
                recv_sem=r1.at[index(offset)],
                device_id=device(0, 1, 0),
                device_id_type=MESH,
            )
            copy.start()
            copies[offset] = copy

    waiting = [(dc, dz) for dc, _, dz in near]
    for t in range(tiles):
        loads[t].wait()
        span = pl.ds(t * rows_tile, rows_tile)
        unit[span] = rms_rows(unit[span])
        if t > 0:
            share = -(-len(waiting) // (tiles - t))
            for dc, dz in waiting[:share]:
                forward(dc, dz)
            waiting = waiting[share:]

    inputs[2].wait()
    for offset in side + twin + far:
        copies[offset].wait_recv()

    line = nz * groups * CAP
    total_rows = ny * line
    rows = every[...].reshape(total_rows, width)

    def score_step(t, total):
        span = pl.ds(t * rows_tile, rows_tile)
        score = lax.dot_general(
            rows, unit[span], (((1,), (1,)), ((), ())), preferred_element_type=jnp.float32
        )
        weight = valid_ref[t].astype(jnp.float32) * jnp.exp(score * (sharp / width))
        low[t] = weight.astype(jnp.bfloat16)
        return total + jnp.sum(weight, axis=1, keepdims=True)

    def halves(mass):
        high = jnp.broadcast_to(mass, (mass.shape[0], 64)).astype(jnp.bfloat16)
        rest = (mass - high.astype(jnp.float32)).astype(jnp.bfloat16)
        return jnp.concatenate([high, rest], axis=1)

    def joined(pair):
        return pair[:, 0:1] + pair[:, 64:65]

    across = {}

    def send_across(k, src, dst):
        if ny == 2:
            copy = pltpu.make_async_remote_copy(
                src_ref=src,
                dst_ref=dst,
                send_sem=sy.at[k],
                recv_sem=ry.at[k],
                device_id=device(0, 1, 0),
                device_id_type=MESH,
            )
            copy.start()
            across[k] = copy

    along = {}

    def send_along(k, src, dst):
        along[k] = []
        for dc, _, dz in near + twin:
            i = k * groups * nz + dc * nz + dz
            copy = pltpu.make_async_remote_copy(
                src_ref=src.at[lax.rem(z + dz, nz), lax.rem(c + dc, groups)],
                dst_ref=dst.at[z, c],
                send_sem=sz.at[i],
                recv_sem=rz.at[i],
                device_id=device(dc, 0, dz),
                device_id_type=MESH,
            )
            copy.start()
            along[k].append(copy)
        dst[z, c] = src[z, c]

    block = (nz, groups, CAP)

    def pass_mass():
        mass = mown[...]
        if ny == 2:
            across[chunks].wait_recv()
            mass += joined(myrecv[...].reshape(line, 128).astype(jnp.float32))
        mzsend[...] = halves(mass).reshape(block + (128,))
        send_along(chunks, mzsend, mzrecv)

    def pass_chunk(k):
        value = own[k]
        if ny == 2:
            across[k].wait_recv()
            value += yrecv[k].astype(jnp.float32).reshape(line, chunk)
        zsend[k] = value.astype(jnp.bfloat16).reshape(block + (chunk,))
        send_along(k, zsend.at[k], zrecv.at[k])

    total = lax.fori_loop(0, tiles, score_step, jnp.zeros((total_rows, 1), jnp.float32))
    mown[...] = total[:line]
    if ny == 2:
        mysend[...] = halves(total[line:]).reshape(block + (128,))
    send_across(chunks, mysend, myrecv)

    def add_up(k, lo, hi):
        summed = jnp.zeros((hi - lo, chunk), jnp.float32)
        for t in range(tiles):
            summed += jnp.dot(
                low[t, lo:hi],
                unit[t * rows_tile : (t + 1) * rows_tile, k * chunk : (k + 1) * chunk],
                preferred_element_type=jnp.float32,
            )
        return summed

    if ny == 2:
        for k in range(chunks):
            summed = add_up(k, line, total_rows)
            ysend[k] = summed.astype(jnp.bfloat16).reshape(block + (chunk,))
            send_across(k, ysend.at[k], yrecv.at[k])
    for k in range(chunks):
        own[k] = add_up(k, 0, line)
        if k == 0:
            pass_mass()
    for k in range(chunks):
        pass_chunk(k)

    def choose(values, rows_last):
        args = (values, picker) if rows_last else (picker, values)
        return lax.dot_general(
            *args, (((0,), (0,)), ((), ())),
            preferred_element_type=jnp.float32, precision=lax.Precision.HIGHEST,
        )

    for copy in along[chunks]:
        copy.wait_recv()
    pairs = jnp.sum(mzrecv[...].astype(jnp.float32), axis=0).reshape(groups * CAP, 128)
    mass = joined(choose(pairs, False))
    column = choose(pairs, True)
    dens_ref[...] = (column[0:1] + column[64:65]) / clu_rows
    for k in range(chunks):
        for copy in along[k]:
            copy.wait_recv()
        sums = jnp.sum(zrecv[k].astype(jnp.float32), axis=0).reshape(groups * CAP, chunk)
        drift_ref[:, k * chunk : (k + 1) * chunk] = (
            (0.5 * math.sqrt(width)) * choose(sums, False) / mass
        )

    for copy in list(copies.values()) + list(across.values()) + sum(along.values(), []):
        copy.wait_send()


def shards(candidates, cluster_ids, pool, pool_valid):
    count, width = candidates.shape
    groups = lax.axis_size("clu")
    slabs = lax.axis_size("slab")
    ny = 2 if slabs % 2 == 0 else 1
    nz = slabs // ny
    pool_rows = pool.shape[0]
    tiles = 2
    peers = groups * slabs
    line = nz * groups * CAP
    chunk = width // CHUNKS
    vmem = pl.BlockSpec(memory_space=pltpu.VMEM)
    hbm = pl.BlockSpec(memory_space=pltpu.HBM)
    dims = (groups, nz, ny, tiles, CHUNKS, float(pool_rows * slabs))
    stage = pltpu.VMEM((CHUNKS, nz, groups, CAP, chunk), jnp.bfloat16)
    small = pltpu.VMEM((nz, groups, CAP, 128), jnp.bfloat16)
    messages = (CHUNKS + 1) * groups * nz
    drift, density = pl.pallas_call(
        functools.partial(kernel, dims),
        out_shape=(
            pltpu.VMEM((count, width), jnp.float32),
            pltpu.VMEM((1, count), jnp.float32),
        ),
        in_specs=[hbm, hbm, hbm, hbm],
        out_specs=(vmem, vmem),
        scratch_shapes=[
            pltpu.VMEM((count, width), jnp.bfloat16),
            pltpu.VMEM((1, count), jnp.int32),
            pltpu.VMEM((tiles, 1, pool_rows // tiles), jnp.int32),
            pltpu.VMEM((pool_rows, width), jnp.bfloat16),
            pltpu.VMEM((groups, CAP, width), jnp.bfloat16),
            pltpu.VMEM((ny, nz, groups, CAP, width), jnp.bfloat16),
            pltpu.VMEM((tiles, peers * CAP, pool_rows // tiles), jnp.bfloat16),
            stage,
            stage,
            pltpu.VMEM((CHUNKS, line, chunk), jnp.float32),
            stage,
            stage,
            small,
            small,
            pltpu.VMEM((line, 1), jnp.float32),
            small,
            small,
            pltpu.SemaphoreType.DMA((3,)),
            pltpu.SemaphoreType.DMA((tiles,)),
            pltpu.SemaphoreType.DMA((peers,)),
            pltpu.SemaphoreType.DMA((peers,)),
            pltpu.SemaphoreType.DMA((CHUNKS + 1,)),
            pltpu.SemaphoreType.DMA((CHUNKS + 1,)),
            pltpu.SemaphoreType.DMA((messages,)),
            pltpu.SemaphoreType.DMA((messages,)),
        ],
        compiler_params=pltpu.CompilerParams(
            collective_id=0, has_side_effects=True, vmem_limit_bytes=63480000
        ),
    )(
        candidates,
        cluster_ids.reshape(1, count),
        pool_valid.reshape(tiles, 1, pool_rows // tiles),
        pool,
    )
    return (drift, density.reshape(count))


def solution(mesh):
    return jax.shard_map(
        shards,
        mesh=mesh,
        in_specs=(
            P(("grp", "clu", "slab"), None),
            P(("grp", "clu", "slab"), None),
            P(("grp", "clu", "slab"), None),
            P(("grp", "clu", "slab")),
        ),
        out_specs=(P(("grp", "clu", "slab"), None), P(("grp", "clu", "slab"))),
        check_vma=False,
    )
```

```python
import functools
import math

import jax
import jax.numpy as jnp
from jax import lax
from jax.experimental import pallas as pl
from jax.experimental.pallas import tpu as pltpu
from jax.sharding import PartitionSpec as P

CAP = 16
PARTS = 2
TILES = 2
FAR_FIRST = False
MESH = pl.DeviceIdType.MESH


def rms_rows(data):
    wide = data.astype(jnp.float32)
    factor = lax.rsqrt(jnp.mean(wide * wide, axis=-1, keepdims=True) + 1e-06)
    return (wide * factor).astype(jnp.bfloat16)


def fold(values, sub):
    half = values.shape[1] // 2
    values = values.reshape(-1, sub, 2 * half)
    return jnp.concatenate([values[..., :half], values[..., half:]], axis=1)


def unfold(values):
    blocks, double, half = values.shape
    sub = double // 2
    values = jnp.concatenate([values[:, :sub], values[:, sub:]], axis=2)
    return values.reshape(blocks * sub, 2 * half)


def kernel(dims, cand_hbm, ids_hbm, valid_hbm, pool_hbm, drift_ref, dens_ref,
           cand_ref, ids_ref, valid_ref, unit, turned, outgoing, every, low,
           ysend, yrecv, own, zsend, zrecv, mysend, myrecv, mzsend, mzrecv,
           in_sem, pool_sem, s1, r1, sy, ry, sz, rz):
    groups, nz, ny, tiles, clu_rows = dims
    count, width = cand_ref.shape
    pool_rows = pool_hbm.shape[0]
    rows_tile = pool_rows // tiles
    sharp = 2.0 * math.sqrt(width)
    sub = CAP // PARTS
    half = width // 2
    c = lax.axis_index("clu")
    slab = lax.axis_index("slab")
    z, y = lax.div(slab, ny), lax.rem(slab, ny)

    def spot(dc, dy, pz):
        return {"clu": lax.rem(c + dc, groups), "slab": pz * ny + lax.rem(y + dy, ny)}

    def device(dc, dy, dz):
        return spot(dc, dy, lax.rem(z + dz, nz))

    def planned(src, dst, send, i, recv, j, where):
        return pltpu.make_async_remote_copy(
            src_ref=src, dst_ref=dst, send_sem=send.at[i], recv_sem=recv.at[j],
            device_id=where, device_id_type=MESH,
        )

    def remote(src, dst, send, recv, i, where):
        copy = planned(src, dst, send, i, recv, i, where)
        copy.start()
        return copy

    hops = sorted(range(1, nz), key=lambda d: (min(d, nz - d), d), reverse=FAR_FIRST)
    near = [(dc, 0, dz) for dz in hops for dc in range(groups)]
    side = [(dc, 1, 0) for dc in range(groups)] if ny == 2 else []
    twin = [(dc, 0, 0) for dc in range(1, groups)]
    far = [(dc, 1, dz) for dz in hops for dc in range(groups)] if ny == 2 else []
    direct = near + side + twin

    def index(b, offset):
        return ((b * groups + offset[0]) * ny + offset[1]) * nz + offset[2]

    inputs = []
    for i, (src, dst) in enumerate(
        [(cand_hbm, cand_ref), (ids_hbm, ids_ref), (valid_hbm, valid_ref)]
    ):
        load = pltpu.make_async_copy(src, dst, in_sem.at[i])
        load.start()
        inputs.append(load)
    loads = []
    for t in range(tiles):
        span = pl.ds(t * rows_tile, rows_tile)
        load = pltpu.make_async_copy(pool_hbm.at[span], unit.at[span], pool_sem.at[t])
        load.start()
        loads.append(load)

    barrier = pltpu.get_barrier_semaphore()
    for offset in direct:
        pl.semaphore_signal(barrier, inc=1, device_id=device(*offset), device_id_type=MESH)

    inputs[0].wait()
    inputs[1].wait()
    ids = ids_ref[...]
    member = (
        lax.broadcasted_iota(jnp.int32, (groups, count), 0) == ids
    ).astype(jnp.float32)
    upper = (
        lax.broadcasted_iota(jnp.int32, (count, count), 0)
        <= lax.broadcasted_iota(jnp.int32, (count, count), 1)
    ).astype(jnp.float32)
    ranks = jnp.dot(member, upper, preferred_element_type=jnp.float32)
    place = (jnp.sum(member * ranks, axis=0, keepdims=True) - 1.0).astype(jnp.int32)

    def one_hot(rows, slot):
        return lax.broadcasted_iota(jnp.int32, (rows, count), 0) == slot

    picker = one_hot(groups * CAP, ids * CAP + place).astype(jnp.float32)
    picks = [
        one_hot(
            groups * sub, jnp.where(place // sub == b, ids * sub + place - b * sub, -1)
        ).astype(jnp.float32)
        for b in range(PARTS)
    ]
    sent = jnp.dot(
        picker.astype(jnp.bfloat16), rms_rows(cand_ref[...]), preferred_element_type=jnp.float32
    )
    sent = fold(sent, sub).astype(jnp.bfloat16)
    for g in range(groups):
        for b in range(PARTS):
            outgoing[b, g] = sent[g * PARTS + b]
    for b in range(PARTS):
        every[b, 0, z, c] = outgoing[b, c]

    pl.semaphore_wait(barrier, len(direct))

    copies = {}
    for b in range(PARTS):
        for offset in direct:
            copies[b, offset] = remote(
                outgoing.at[b, lax.rem(c + offset[0], groups)],
                every.at[b, offset[1], z, c],
                s1, r1, index(b, offset), device(*offset),
            )

    for t in range(tiles):
        loads[t].wait()
        span = pl.ds(t * rows_tile, rows_tile)
        value = rms_rows(unit[span])
        unit[span] = value
        turned[t] = value.T
    inputs[2].wait()

    for b in range(PARTS):
        for dc, _, dz in near:
            copies[b, (dc, 0, dz)].wait_recv()
            if ny == 2:
                fc, fz = lax.rem(c + groups - dc, groups), lax.rem(z + nz - dz, nz)
                block = every.at[b, 0, fz, fc]
                copies[b, (dc, 1, dz)] = remote(
                    block, every.at[b, 1, fz, fc],
                    s1, r1, index(b, (dc, 1, dz)), device(0, 1, 0),
                )

    line = nz * groups * sub
    total_rows = ny * line

    def score(b):
        rows = unfold(
            every[b].reshape(ny * nz * groups, 2 * sub, half).astype(jnp.float32)
        ).astype(jnp.bfloat16)
        total = jnp.zeros((total_rows, 1), jnp.float32)
        for t in range(tiles):
            dots = jnp.dot(rows, turned[t], preferred_element_type=jnp.float32)
            weight = valid_ref[t].astype(jnp.float32) * jnp.exp(dots * (sharp / width))
            low[t] = weight.astype(jnp.bfloat16)
            total += jnp.sum(weight, axis=1, keepdims=True)
        return total.reshape(ny, nz * groups, sub, 1)

    def add_up():
        summed = jnp.zeros((total_rows, width), jnp.float32)
        for t in range(tiles):
            summed += jnp.dot(
                low[t], unit[t * rows_tile : (t + 1) * rows_tile],
                preferred_element_type=jnp.float32,
            )
        return fold(summed, sub).reshape(ny, nz, groups, 2 * sub, half)

    def halves(mass):
        high = jnp.broadcast_to(mass, mass.shape[:-1] + (64,)).astype(jnp.bfloat16)
        rest = (mass - high.astype(jnp.float32)).astype(jnp.bfloat16)
        return jnp.concatenate([high, rest], axis=-1).reshape(nz, groups, CAP, 128)

    def joined(pair):
        return pair[..., 0:1] + pair[..., 64:65]

    me = z * groups + c
    sources = [(dz, dc) for dz in range(nz) for dc in range(groups) if (dz, dc) != (0, 0)]
    turns = sum(([a, nz - 1 - a] for a in range((nz + 1) // 2)), [])[:nz]
    across = {}

    def outward(b, pz, dc):
        pc = lax.rem(c + dc, groups)
        src, dst = (mzsend, mzrecv) if b == PARTS else (zsend.at[b], zrecv.at[b])
        at = b * nz * groups
        return planned(
            src.at[pz, pc], dst.at[z, c], sz, at + pz * groups + pc, rz, at + me,
            spot(dc, 0, pz),
        )

    def pass_on(b, pz):
        src, dst = (mzsend, mzrecv) if b == PARTS else (zsend.at[b], zrecv.at[b])

        @pl.when(z != pz)
        def _():
            outward(b, pz, 0).start()

        @pl.when(z == pz)
        def _():
            dst[z, c] = src[pz, c]

        for dc in range(1, groups):
            outward(b, pz, dc).start()

    def collect(b):
        for dz, dc in sources:
            pz, pc = lax.rem(z + dz, nz), lax.rem(c + dc, groups)
            dst = mzrecv if b == PARTS else zrecv.at[b]
            j = (b * nz + pz) * groups + pc
            planned(dst.at[pz, pc], dst.at[pz, pc], sz, j, rz, j, spot(dc, 0, pz)).wait_recv()

    totals = []
    for b in range(PARTS):
        for offset in side + twin + far:
            copies[b, offset].wait_recv()
        totals.append(score(b))
        if b == PARTS - 1:
            mass = jnp.concatenate(totals, axis=2)
            if ny == 2:
                mysend[...] = halves(mass[1])
                across["mass"] = remote(mysend, myrecv, sy, ry, PARTS * nz, device(0, 1, 0))
        summed = add_up()
        if ny == 2:
            ysend[b] = summed[1].astype(jnp.bfloat16)
            for pz in turns:
                across[b, pz] = remote(
                    ysend.at[b, pz], yrecv.at[b, pz], sy, ry, b * nz + pz, device(0, 1, 0)
                )
        own[b] = summed[0]

    for b in range(PARTS):
        for pz in turns:
            value = own[b, pz]
            if ny == 2:
                across[b, pz].wait_recv()
                value += yrecv[b, pz].astype(jnp.float32)
            zsend[b, pz] = value.astype(jnp.bfloat16)
            pass_on(b, pz)
        if b == 0:
            value = mass[0].reshape(nz, groups, CAP, 1)
            if ny == 2:
                across["mass"].wait_recv()
                value += joined(myrecv[...].astype(jnp.float32))
            mzsend[...] = halves(value)
            for pz in turns:
                pass_on(PARTS, pz)

    def choose(pick, values, rows_last=False):
        args = (values, pick) if rows_last else (pick, values)
        return lax.dot_general(
            *args, (((0,), (0,)), ((), ())),
            preferred_element_type=jnp.float32, precision=lax.Precision.HIGHEST,
        )

    drift = jnp.zeros((count, width), jnp.float32)
    for b in range(PARTS):
        collect(b)
        sums = unfold(jnp.sum(zrecv[b].astype(jnp.float32), axis=0))
        drift += choose(picks[b], sums)
        if b == 0:
            collect(PARTS)
            pairs = jnp.sum(mzrecv[...].astype(jnp.float32), axis=0).reshape(groups * CAP, 128)
            scale = (0.5 * math.sqrt(width)) / joined(choose(picker, pairs))
            column = choose(picker, pairs, True)
            dens_ref[...] = (column[0:1] + column[64:65]) / clu_rows
    drift_ref[...] = drift * scale

    for copy in list(copies.values()) + list(across.values()):
        copy.wait_send()
    for b in range(PARTS + 1):
        for dz, dc in sources:
            outward(b, lax.rem(z + dz, nz), dc).wait_send()


def shards(candidates, cluster_ids, pool, pool_valid):
    count, width = candidates.shape
    groups = lax.axis_size("clu")
    slabs = lax.axis_size("slab")
    ny = 2 if slabs % 2 == 0 else 1
    nz = slabs // ny
    pool_rows = pool.shape[0]
    tiles = TILES
    peers = groups * slabs
    half = width // 2
    sub = CAP // PARTS
    vmem = pl.BlockSpec(memory_space=pltpu.VMEM)
    hbm = pl.BlockSpec(memory_space=pltpu.HBM)
    dims = (groups, nz, ny, tiles, float(pool_rows * slabs))
    stage = pltpu.VMEM((PARTS, nz, groups, 2 * sub, half), jnp.bfloat16)
    small = pltpu.VMEM((nz, groups, CAP, 128), jnp.bfloat16)
    sem = pltpu.SemaphoreType.DMA
    drift, density = pl.pallas_call(
        functools.partial(kernel, dims),
        out_shape=(
            pltpu.VMEM((count, width), jnp.float32),
            pltpu.VMEM((1, count), jnp.float32),
        ),
        in_specs=[hbm, hbm, hbm, hbm],
        out_specs=(vmem, vmem),
        scratch_shapes=[
            pltpu.VMEM((count, width), jnp.bfloat16),
            pltpu.VMEM((1, count), jnp.int32),
            pltpu.VMEM((tiles, 1, pool_rows // tiles), jnp.int32),
            pltpu.VMEM((pool_rows, width), jnp.bfloat16),
            pltpu.VMEM((tiles, width, pool_rows // tiles), jnp.bfloat16),
            pltpu.VMEM((PARTS, groups, 2 * sub, half), jnp.bfloat16),
            pltpu.VMEM((PARTS, ny, nz, groups, 2 * sub, half), jnp.bfloat16),
            pltpu.VMEM((tiles, peers * sub, pool_rows // tiles), jnp.bfloat16),
            stage,
            stage,
            pltpu.VMEM((PARTS, nz, groups, 2 * sub, half), jnp.float32),
            stage,
            stage,
            small,
            small,
            small,
            small,
            sem((3,)),
            sem((tiles,)),
            sem((PARTS * peers,)),
            sem((PARTS * peers,)),
            sem((PARTS * nz + 1,)),
            sem((PARTS * nz + 1,)),
            sem(((PARTS + 1) * nz * groups,)),
            sem(((PARTS + 1) * nz * groups,)),
        ],
        compiler_params=pltpu.CompilerParams(
            collective_id=0, has_side_effects=True, vmem_limit_bytes=63480000
        ),
    )(
        candidates,
        cluster_ids.reshape(1, count),
        pool_valid.reshape(tiles, 1, pool_rows // tiles),
        pool,
    )
    return (drift, density.reshape(count))


def solution(mesh):
    return jax.shard_map(
        shards,
        mesh=mesh,
        in_specs=(
            P(("grp", "clu", "slab"), None),
            P(("grp", "clu", "slab"), None),
            P(("grp", "clu", "slab"), None),
            P(("grp", "clu", "slab")),
        ),
        out_specs=(P(("grp", "clu", "slab"), None), P(("grp", "clu", "slab"))),
        check_vma=False,
    )
```

```python
import functools
import math

import jax
import jax.numpy as jnp
from jax import lax
from jax.experimental import pallas as pl
from jax.experimental.pallas import tpu as pltpu
from jax.sharding import PartitionSpec as P

CAP = 16
PARTS = 2
TILES = 2
FAR_FIRST = False
MESH = pl.DeviceIdType.MESH


def rms_rows(data):
    wide = data.astype(jnp.float32)
    factor = lax.rsqrt(jnp.mean(wide * wide, axis=-1, keepdims=True) + 1e-06)
    return (wide * factor).astype(jnp.bfloat16)


def fold(values, sub):
    half = values.shape[1] // 2
    values = values.reshape(-1, sub, 2 * half)
    return jnp.concatenate([values[..., :half], values[..., half:]], axis=1)


def unfold(values):
    blocks, double, half = values.shape
    sub = double // 2
    values = jnp.concatenate([values[:, :sub], values[:, sub:]], axis=2)
    return values.reshape(blocks * sub, 2 * half)


def kernel(dims, cand_hbm, ids_hbm, valid_hbm, pool_hbm, drift_ref, dens_ref,
           cand_ref, ids_ref, valid_ref, unit, turned, outgoing, every, low,
           *rest):
    ysend, yrecv, own, zsend, zrecv = (rest[i * PARTS : (i + 1) * PARTS] for i in range(5))
    in_sem, pool_sem, s1, r1, s2, r2, sy, ry, sz, rz = rest[5 * PARTS :]
    groups, nz, ny, tiles, clu_rows = dims
    count, width = cand_ref.shape
    pool_rows = pool_hbm.shape[0]
    rows_tile = pool_rows // tiles
    sharp = 2.0 * math.sqrt(width)
    sub = CAP // PARTS
    half = width // 2
    c = lax.axis_index("clu")
    slab = lax.axis_index("slab")
    z, y = lax.div(slab, ny), lax.rem(slab, ny)

    def spot(dc, dy, pz):
        return {"clu": lax.rem(c + dc, groups), "slab": pz * ny + lax.rem(y + dy, ny)}

    def device(dc, dy, dz):
        return spot(dc, dy, lax.rem(z + dz, nz))

    def planned(src, dst, send, i, recv, j, where):
        return pltpu.make_async_remote_copy(
            src_ref=src, dst_ref=dst, send_sem=send.at[i], recv_sem=recv.at[j],
            device_id=where, device_id_type=MESH,
        )

    def remote(src, dst, send, recv, i, where):
        copy = planned(src, dst, send, i, recv, i, where)
        copy.start()
        return copy

    hops = sorted(range(1, nz), key=lambda d: (min(d, nz - d), d), reverse=FAR_FIRST)
    near = [(dc, 0, dz) for dz in hops for dc in range(groups)]
    side = [(dc, 1, 0) for dc in range(groups)] if ny == 2 else []
    twin = [(dc, 0, 0) for dc in range(1, groups)]
    direct = near + side + twin

    def index(b, offset):
        return ((b * groups + offset[0]) * ny + offset[1]) * nz + offset[2]

    inputs = []
    for i, (src, dst) in enumerate(
        [(cand_hbm, cand_ref), (ids_hbm, ids_ref), (valid_hbm, valid_ref)]
    ):
        load = pltpu.make_async_copy(src, dst, in_sem.at[i])
        load.start()
        inputs.append(load)
    loads = []
    for t in range(tiles):
        span = pl.ds(t * rows_tile, rows_tile)
        load = pltpu.make_async_copy(pool_hbm.at[span], unit.at[span], pool_sem.at[t])
        load.start()
        loads.append(load)

    barrier = pltpu.get_barrier_semaphore()
    for offset in direct:
        pl.semaphore_signal(barrier, inc=1, device_id=device(*offset), device_id_type=MESH)

    inputs[0].wait()
    inputs[1].wait()
    ids = ids_ref[...]
    member = (
        lax.broadcasted_iota(jnp.int32, (groups, count), 0) == ids
    ).astype(jnp.float32)
    upper = (
        lax.broadcasted_iota(jnp.int32, (count, count), 0)
        <= lax.broadcasted_iota(jnp.int32, (count, count), 1)
    ).astype(jnp.float32)
    ranks = jnp.dot(member, upper, preferred_element_type=jnp.float32)
    place = (jnp.sum(member * ranks, axis=0, keepdims=True) - 1.0).astype(jnp.int32)

    def one_hot(rows, slot):
        return lax.broadcasted_iota(jnp.int32, (rows, count), 0) == slot

    lower = jnp.sum(member[0:1], axis=1, keepdims=True).astype(jnp.int32)
    rank = jnp.where(ids == 0, place, place + lower)
    shared = (rank >= sub) & (rank < CAP)
    inner = jnp.where(rank >= CAP, rank - CAP, jnp.where(shared, rank - sub, rank))
    picker = one_hot(
        groups * CAP, ids * CAP + jnp.where(shared, sub, 0) + inner
    ).astype(jnp.float32)
    picks = [
        one_hot(groups * sub, jnp.where(shared == (b == 1), ids * sub + inner, -1))
        for b in range(PARTS)
    ]
    sent = jnp.dot(
        one_hot(count, rank).astype(jnp.bfloat16), rms_rows(cand_ref[...]),
        preferred_element_type=jnp.float32,
    )
    outgoing[...] = fold(sent, sub).astype(jnp.bfloat16)
    every[0, 0, z, c] = outgoing[2 * c]
    every[1, 0, z, c] = outgoing[1]

    pl.semaphore_wait(barrier, len(direct))

    copies, twins = {}, {}

    def spread(b, offset):
        src = outgoing.at[1] if b else outgoing.at[2 * lax.rem(c + offset[0], groups)]
        copies[b, offset] = remote(
            src, every.at[b, offset[1], z, c], s1, r1, index(b, offset), device(*offset)
        )

    def hand_over(dy, dz):
        block = every.at[1, dy, lax.rem(z + nz - dz, nz), c]
        twins[dy, dz] = remote(block, block, s2, r2, dy * nz + dz, spot(1, 0, z))

    for offset in direct:
        spread(0, offset)
    for t in range(tiles):
        loads[t].wait()
        span = pl.ds(t * rows_tile, rows_tile)
        value = rms_rows(unit[span])
        unit[span] = value
        turned[t] = value.T
        if t == 0:
            for offset in direct:
                if offset[0] == 0:
                    spread(1, offset)
            hand_over(0, 0)
    inputs[2].wait()

    for b in range(PARTS):
        for dz in hops:
            for dc in range(groups if b == 0 else 1):
                copies[b, (dc, 0, dz)].wait_recv()
                if ny == 2:
                    fz = lax.rem(z + nz - dz, nz)
                    fc = lax.rem(c + groups - dc, groups)
                    copies[b, (dc, 1, dz)] = remote(
                        every.at[b, 0, fz, fc], every.at[b, 1, fz, fc],
                        s1, r1, index(b, (dc, 1, dz)), device(0, 1, 0),
                    )
                if b == 1:
                    hand_over(0, dz)

    line = nz * groups * sub
    total_rows = ny * line

    def score(b):
        rows = unfold(
            every[b].reshape(ny * nz * groups, 2 * sub, half).astype(jnp.float32)
        ).astype(jnp.bfloat16)
        total = jnp.zeros((total_rows, 1), jnp.float32)
        for t in range(tiles):
            dots = jnp.dot(rows, turned[t], preferred_element_type=jnp.float32)
            weight = valid_ref[t].astype(jnp.float32) * jnp.exp(dots * (sharp / width))
            low[t] = weight.astype(jnp.bfloat16)
            total += jnp.sum(weight, axis=1, keepdims=True)
        return total.reshape(ny, nz * groups, sub, 1)

    def add_up():
        summed = jnp.zeros((total_rows, width), jnp.float32)
        for t in range(tiles):
            summed += jnp.dot(
                low[t], unit[t * rows_tile : (t + 1) * rows_tile],
                preferred_element_type=jnp.float32,
            )
        return fold(summed, sub).reshape(ny, nz, groups, 2 * sub, half)

    def halves(mass):
        high = jnp.broadcast_to(mass, mass.shape[:-1] + (64,)).astype(jnp.bfloat16)
        rest = (mass - high.astype(jnp.float32)).astype(jnp.bfloat16)
        return jnp.concatenate([high, rest], axis=-1)

    def joined(pair):
        return pair[..., 0:1] + pair[..., 64:65]

    me = z * groups + c
    sources = [(dz, dc) for dz in range(nz) for dc in range(groups) if (dz, dc) != (0, 0)]
    turns = sum(([a, nz - 1 - a] for a in range((nz + 1) // 2)), [])[:nz]
    across = {}

    reach = 1
    last = PARTS - 1

    def outward(b, pz, dc):
        pc = lax.rem(c + dc, groups)
        at = b * nz * groups
        return planned(
            zsend[b].at[pz, pc], zrecv[b].at[z, c], sz, at + pz * groups + pc, rz, at + me,
            spot(dc, 0, pz),
        )

    def pass_on(b, pz):
        @pl.when(z != pz)
        def _():
            outward(b, pz, 0).start()

        @pl.when(z == pz)
        def _():
            zrecv[b][z, c] = zsend[b][pz, c]

        for dc in range(1, groups):
            outward(b, pz, dc).start()

    def collect(b):
        for dz, dc in sources:
            pz, pc = lax.rem(z + dz, nz), lax.rem(c + dc, groups)
            block = zrecv[b].at[pz, pc]
            j = (b * nz + pz) * groups + pc
            planned(block, block, sz, j, rz, j, spot(dc, 0, pz)).wait_recv()

    totals = []
    for b in range(PARTS):
        if b == 0:
            for offset in side + twin:
                copies[b, offset].wait_recv()
            if ny == 2:
                for dz in hops:
                    for dc in range(groups):
                        copies[b, (dc, 1, dz)].wait_recv()
        else:
            for copy in twins.values():
                copy.wait_recv()
        totals.append(score(b))
        if b == 0 and ny == 2:
            for dz in [0] + hops:
                copies[1, (0, 1, dz)].wait_recv()
                hand_over(1, dz)
        summed = add_up()
        if b == last:
            mass = jnp.concatenate(totals, axis=2).reshape(ny, nz, groups, CAP, 1)
        if ny == 2:
            for k, pz in enumerate(turns):
                ysend[b][k, :, :, :half] = summed[1, pz].astype(jnp.bfloat16)
                if b == last:
                    ysend[b][k, :, :, half:] = halves(mass[1, pz])
                if (k + 1) % reach == 0 or k == nz - 1:
                    lo = k // reach * reach
                    span = pl.ds(lo, k + 1 - lo)
                    across[b, lo] = remote(
                        ysend[b].at[span], yrecv[b].at[span],
                        sy, ry, b * nz + lo, spot(0, 1, z),
                    )
        own[b][...] = summed[0]

    for b in range(PARTS):
        for k, pz in enumerate(turns):
            value = own[b][pz]
            if ny == 2:
                if k % reach == 0:
                    across[b, k].wait_recv()
                value += yrecv[b][k, :, :, :half].astype(jnp.float32)
            zsend[b][pz, :, :, :half] = value.astype(jnp.bfloat16)
            if b == last:
                value = mass[0, pz]
                if ny == 2:
                    value += joined(yrecv[b][k, :, :, half:].astype(jnp.float32))
                zsend[b][pz, :, :, half:] = halves(value)
            pass_on(b, pz)

    def choose(pick, values):
        pick = pick.astype(jnp.bfloat16)
        high = values.astype(jnp.bfloat16)
        rest = (values - high.astype(jnp.float32)).astype(jnp.bfloat16)
        return sum(
            lax.dot_general(
                pick, x, (((0,), (0,)), ((), ())), preferred_element_type=jnp.float32
            )
            for x in (high, rest)
        )

    for copy in list(copies.values()) + list(twins.values()) + list(across.values()):
        copy.wait_send()
    drift = jnp.zeros((count, width), jnp.float32)
    for b in range(PARTS):
        collect(b)
        if b == last:
            pairs = jnp.sum(zrecv[b][..., half:].astype(jnp.float32), axis=0)
            pairs = pairs.reshape(groups * CAP, 128)
            total = joined(lax.dot_general(
                picker, pairs, (((0,), (0,)), ((), ())),
                preferred_element_type=jnp.float32, precision=lax.Precision.HIGHEST,
            ))
            column = lax.dot_general(
                pairs, picker, (((0,), (0,)), ((), ())),
                preferred_element_type=jnp.float32, precision=lax.Precision.HIGHEST,
            )
            dens_ref[...] = (column[0:1] + column[64:65]) / clu_rows
        sums = unfold(jnp.sum(zrecv[b][..., :half].astype(jnp.float32), axis=0))
        drift += choose(picks[b], sums)
        if b < last:
            for dz, dc in sources:
                outward(b, lax.rem(z + dz, nz), dc).wait_send()
    drift_ref[...] = drift * ((0.5 * math.sqrt(width)) / total)
    for dz, dc in sources:
        outward(last, lax.rem(z + dz, nz), dc).wait_send()


def shards(candidates, cluster_ids, pool, pool_valid):
    count, width = candidates.shape
    groups = lax.axis_size("clu")
    slabs = lax.axis_size("slab")
    ny = 2 if slabs % 2 == 0 else 1
    nz = slabs // ny
    pool_rows = pool.shape[0]
    tiles = TILES
    peers = groups * slabs
    half = width // 2
    sub = CAP // PARTS
    vmem = pl.BlockSpec(memory_space=pltpu.VMEM)
    hbm = pl.BlockSpec(memory_space=pltpu.HBM)
    dims = (groups, nz, ny, tiles, float(pool_rows * slabs))
    stages = [
        pltpu.VMEM((nz, groups, 2 * sub, half + (128 if b == PARTS - 1 else 0)), jnp.bfloat16)
        for b in range(PARTS)
    ]
    held = pltpu.VMEM((nz, groups, 2 * sub, half), jnp.float32)
    sem = pltpu.SemaphoreType.DMA
    drift, density = pl.pallas_call(
        functools.partial(kernel, dims),
        out_shape=(
            pltpu.VMEM((count, width), jnp.float32),
            pltpu.VMEM((1, count), jnp.float32),
        ),
        in_specs=[hbm, hbm, hbm, hbm],
        out_specs=(vmem, vmem),
        scratch_shapes=[
            pltpu.VMEM((count, width), jnp.bfloat16),
            pltpu.VMEM((1, count), jnp.int32),
            pltpu.VMEM((tiles, 1, pool_rows // tiles), jnp.int32),
            pltpu.VMEM((pool_rows, width), jnp.bfloat16),
            pltpu.VMEM((tiles, width, pool_rows // tiles), jnp.bfloat16),
            pltpu.VMEM((count // sub, 2 * sub, half), jnp.bfloat16),
            pltpu.VMEM((PARTS, ny, nz, groups, 2 * sub, half), jnp.bfloat16),
            pltpu.VMEM((tiles, peers * sub, pool_rows // tiles), jnp.bfloat16),
            *stages,
            *stages,
            *[held] * PARTS,
            *stages,
            *stages,
            sem((3,)),
            sem((tiles,)),
            sem((PARTS * peers,)),
            sem((PARTS * peers,)),
            sem((ny * nz,)),
            sem((ny * nz,)),
            sem((PARTS * nz,)),
            sem((PARTS * nz,)),
            sem((PARTS * nz * groups,)),
            sem((PARTS * nz * groups,)),
        ],
        compiler_params=pltpu.CompilerParams(
            collective_id=0, has_side_effects=True, vmem_limit_bytes=63480000
        ),
    )(
        candidates,
        cluster_ids.reshape(1, count),
        pool_valid.reshape(tiles, 1, pool_rows // tiles),
        pool,
    )
    return (drift, density.reshape(count))


def solution(mesh):
    return jax.shard_map(
        shards,
        mesh=mesh,
        in_specs=(
            P(("grp", "clu", "slab"), None),
            P(("grp", "clu", "slab"), None),
            P(("grp", "clu", "slab"), None),
            P(("grp", "clu", "slab")),
        ),
        out_specs=(P(("grp", "clu", "slab"), None), P(("grp", "clu", "slab"))),
        check_vma=False,
    )
```

```python
import functools
import math

import jax
import jax.numpy as jnp
from jax import lax
from jax.experimental import pallas as pl
from jax.experimental.pallas import tpu as pltpu
from jax.sharding import PartitionSpec as P

CAP = 16
PARTS = 2
TILES = 2
MESH = pl.DeviceIdType.MESH


def rms_rows(data):
    wide = data.astype(jnp.float32)
    factor = lax.rsqrt(jnp.mean(wide * wide, axis=-1, keepdims=True) + 1e-06)
    return (wide * factor).astype(jnp.bfloat16)


def fold(values, sub):
    half = values.shape[1] // 2
    values = values.reshape(-1, sub, 2 * half)
    return jnp.concatenate([values[..., :half], values[..., half:]], axis=1)


def unfold(values):
    blocks, double, half = values.shape
    sub = double // 2
    values = jnp.concatenate([values[:, :sub], values[:, sub:]], axis=2)
    return values.reshape(blocks * sub, 2 * half)


def kernel(dims, cand_hbm, ids_hbm, valid_hbm, pool_hbm, drift_ref, dens_ref,
           cand_ref, ids_ref, valid_ref, unit, turned, outgoing, every, low,
           *rest):
    ysend, yrecv, own, zsend, zrecv = (rest[i * PARTS : (i + 1) * PARTS] for i in range(5))
    in_sem, pool_sem, s1, r1, s2, r2, sy, ry, sz, rz = rest[5 * PARTS :]
    groups, nz, ny, tiles, clu_rows = dims
    count, width = cand_ref.shape
    pool_rows = pool_hbm.shape[0]
    rows_tile = pool_rows // tiles
    sharp = 2.0 * math.sqrt(width)
    sub = CAP // PARTS
    half = width // 2
    c = lax.axis_index("clu")
    slab = lax.axis_index("slab")
    z, y = lax.div(slab, ny), lax.rem(slab, ny)

    def spot(dc, dy, pz):
        return {"clu": lax.rem(c + dc, groups), "slab": pz * ny + lax.rem(y + dy, ny)}

    paired = nz & (nz - 1) == 0

    def partner(dz, back=False):
        if not paired:
            return lax.rem(z + (nz - dz if back else dz), nz)
        place, bit = z, 1
        while bit <= dz:
            if dz & bit:
                place = place + bit - 2 * bit * lax.rem(lax.div(z, bit), 2)
            bit *= 2
        return place

    def device(dc, dy, dz):
        return spot(dc, dy, partner(dz))

    def planned(src, dst, send, i, recv, j, where):
        return pltpu.make_async_remote_copy(
            src_ref=src, dst_ref=dst, send_sem=send.at[i], recv_sem=recv.at[j],
            device_id=where, device_id_type=MESH,
        )

    def remote(src, dst, send, recv, i, where):
        copy = planned(src, dst, send, i, recv, i, where)
        copy.start()
        return copy

    hops = sorted(range(1, nz), key=lambda d: (1 - d % 2, d))
    near = [(dc, 0, dz) for dz in hops for dc in range(groups)]
    side = [(dc, 1, 0) for dc in range(groups)] if ny == 2 else []
    twin = [(dc, 0, 0) for dc in range(1, groups)]
    direct = near + side + twin

    def index(b, offset):
        return ((b * groups + offset[0]) * ny + offset[1]) * nz + offset[2]

    inputs = []
    for i, (src, dst) in enumerate(
        [(cand_hbm, cand_ref), (ids_hbm, ids_ref), (valid_hbm, valid_ref)]
    ):
        load = pltpu.make_async_copy(src, dst, in_sem.at[i])
        load.start()
        inputs.append(load)
    loads = []
    for t in range(tiles):
        span = pl.ds(t * rows_tile, rows_tile)
        load = pltpu.make_async_copy(pool_hbm.at[span], unit.at[span], pool_sem.at[t])
        load.start()
        loads.append(load)

    barrier = pltpu.get_barrier_semaphore()
    for offset in direct:
        pl.semaphore_signal(barrier, inc=1, device_id=device(*offset), device_id_type=MESH)

    inputs[0].wait()
    inputs[1].wait()
    ids = ids_ref[...]
    member = (
        lax.broadcasted_iota(jnp.int32, (groups, count), 0) == ids
    ).astype(jnp.float32)
    upper = (
        lax.broadcasted_iota(jnp.int32, (count, count), 0)
        <= lax.broadcasted_iota(jnp.int32, (count, count), 1)
    ).astype(jnp.float32)
    ranks = jnp.dot(member, upper, preferred_element_type=jnp.float32)
    place = (jnp.sum(member * ranks, axis=0, keepdims=True) - 1.0).astype(jnp.int32)

    def one_hot(rows, slot):
        return lax.broadcasted_iota(jnp.int32, (rows, count), 0) == slot

    lower = jnp.sum(member[0:1], axis=1, keepdims=True).astype(jnp.int32)
    rank = jnp.where(ids == 0, place, place + lower)
    shared = (rank >= sub) & (rank < CAP)
    inner = jnp.where(rank >= CAP, rank - CAP, jnp.where(shared, rank - sub, rank))
    picker = one_hot(
        groups * CAP, ids * CAP + jnp.where(shared, sub, 0) + inner
    ).astype(jnp.float32)
    picks = [
        one_hot(groups * sub, jnp.where(shared == (b == 1), ids * sub + inner, -1))
        for b in range(PARTS)
    ]
    sent = jnp.dot(
        one_hot(count, rank).astype(jnp.bfloat16), rms_rows(cand_ref[...]),
        preferred_element_type=jnp.float32,
    )
    outgoing[...] = fold(sent, sub).astype(jnp.bfloat16)
    every[0, 0, z, c] = outgoing[2 * c]
    every[1, 0, z, c] = outgoing[1]

    pl.semaphore_wait(barrier, len(direct))

    copies, twins = {}, {}

    def spread(b, offset):
        src = outgoing.at[1] if b else outgoing.at[2 * lax.rem(c + offset[0], groups)]
        copies[b, offset] = remote(
            src, every.at[b, offset[1], z, c], s1, r1, index(b, offset), device(*offset)
        )

    def hand_over(dy, dz):
        block = every.at[1, dy, partner(dz, True), c]
        twins[dy, dz] = remote(block, block, s2, r2, dy * nz + dz, spot(1, 0, z))

    for offset in direct:
        spread(0, offset)
    for t in range(tiles):
        loads[t].wait()
        span = pl.ds(t * rows_tile, rows_tile)
        value = rms_rows(unit[span])
        unit[span] = value
        turned[t] = value.T
        if t == 0:
            for offset in direct:
                if offset[0] == 0:
                    spread(1, offset)
            hand_over(0, 0)
    inputs[2].wait()

    for b in range(PARTS):
        for dz in hops:
            for dc in range(groups if b == 0 else 1):
                copies[b, (dc, 0, dz)].wait_recv()
                if ny == 2:
                    fz = partner(dz, True)
                    fc = lax.rem(c + groups - dc, groups)
                    copies[b, (dc, 1, dz)] = remote(
                        every.at[b, 0, fz, fc], every.at[b, 1, fz, fc],
                        s1, r1, index(b, (dc, 1, dz)), device(0, 1, 0),
                    )
                if b == 1:
                    hand_over(0, dz)

    line = nz * groups * sub
    total_rows = ny * line

    def score(b):
        rows = unfold(
            every[b].reshape(ny * nz * groups, 2 * sub, half).astype(jnp.float32)
        ).astype(jnp.bfloat16)
        total = jnp.zeros((total_rows, 1), jnp.float32)
        for t in range(tiles):
            dots = jnp.dot(rows, turned[t], preferred_element_type=jnp.float32)
            weight = valid_ref[t].astype(jnp.float32) * jnp.exp(dots * (sharp / width))
            low[t] = weight.astype(jnp.bfloat16)
            total += jnp.sum(weight, axis=1, keepdims=True)
        return total.reshape(ny, nz * groups, sub, 1)

    def add_up():
        summed = jnp.zeros((total_rows, width), jnp.float32)
        for t in range(tiles):
            summed += jnp.dot(
                low[t], unit[t * rows_tile : (t + 1) * rows_tile],
                preferred_element_type=jnp.float32,
            )
        return fold(summed, sub).reshape(ny, nz, groups, 2 * sub, half)

    def halves(mass):
        high = jnp.broadcast_to(mass, mass.shape[:-1] + (64,)).astype(jnp.bfloat16)
        rest = (mass - high.astype(jnp.float32)).astype(jnp.bfloat16)
        return jnp.concatenate([high, rest], axis=-1)

    def joined(pair):
        return pair[..., 0:1] + pair[..., 64:65]

    me = z * groups + c
    sources = [(dz, dc) for dz in range(nz) for dc in range(groups) if (dz, dc) != (0, 0)]
    turns = sum(([a, nz - 1 - a] for a in range((nz + 1) // 2)), [])[:nz]
    across = {}

    reach = 1
    last = PARTS - 1

    def outward(b, pz, dc):
        pc = lax.rem(c + dc, groups)
        at = b * nz * groups
        return planned(
            zsend[b].at[pz, pc], zrecv[b].at[z, c], sz, at + pz * groups + pc, rz, at + me,
            spot(dc, 0, pz),
        )

    def pass_on(b, pz):
        @pl.when(z != pz)
        def _():
            outward(b, pz, 0).start()

        @pl.when(z == pz)
        def _():
            zrecv[b][z, c] = zsend[b][pz, c]

        for dc in range(1, groups):
            outward(b, pz, dc).start()

    def collect(b):
        for dz, dc in sources:
            pz, pc = lax.rem(z + dz, nz), lax.rem(c + dc, groups)
            block = zrecv[b].at[pz, pc]
            j = (b * nz + pz) * groups + pc
            planned(block, block, sz, j, rz, j, spot(dc, 0, pz)).wait_recv()

    totals = []
    for b in range(PARTS):
        if b == 0:
            for offset in side + twin:
                copies[b, offset].wait_recv()
            if ny == 2:
                for dz in hops:
                    for dc in range(groups):
                        copies[b, (dc, 1, dz)].wait_recv()
        else:
            for copy in twins.values():
                copy.wait_recv()
        totals.append(score(b))
        if b == 0 and ny == 2:
            for dz in [0] + hops:
                copies[1, (0, 1, dz)].wait_recv()
                hand_over(1, dz)
        summed = add_up()
        if b == last:
            mass = jnp.concatenate(totals, axis=2).reshape(ny, nz, groups, CAP, 1)
        if ny == 2:
            for k, pz in enumerate(turns):
                ysend[b][k, :, :, :half] = summed[1, pz].astype(jnp.bfloat16)
                if b == last:
                    ysend[b][k, :, :, half:] = halves(mass[1, pz])
                if (k + 1) % reach == 0 or k == nz - 1:
                    lo = k // reach * reach
                    span = pl.ds(lo, k + 1 - lo)
                    across[b, lo] = remote(
                        ysend[b].at[span], yrecv[b].at[span],
                        sy, ry, b * nz + lo, spot(0, 1, z),
                    )
        own[b][...] = summed[0]

    for b in range(PARTS):
        for k, pz in enumerate(turns):
            value = own[b][pz]
            if ny == 2:
                if k % reach == 0:
                    across[b, k].wait_recv()
                value += yrecv[b][k, :, :, :half].astype(jnp.float32)
            zsend[b][pz, :, :, :half] = value.astype(jnp.bfloat16)
            if b == last:
                value = mass[0, pz]
                if ny == 2:
                    value += joined(yrecv[b][k, :, :, half:].astype(jnp.float32))
                zsend[b][pz, :, :, half:] = halves(value)
            pass_on(b, pz)

    def choose(pick, values):
        pick = pick.astype(jnp.bfloat16)
        high = values.astype(jnp.bfloat16)
        rest = (values - high.astype(jnp.float32)).astype(jnp.bfloat16)
        return sum(
            lax.dot_general(
                pick, x, (((0,), (0,)), ((), ())), preferred_element_type=jnp.float32
            )
            for x in (high, rest)
        )

    for copy in list(copies.values()) + list(twins.values()) + list(across.values()):
        copy.wait_send()
    drift = jnp.zeros((count, width), jnp.float32)
    for b in range(PARTS):
        collect(b)
        if b == last:
            pairs = jnp.sum(zrecv[b][..., half:].astype(jnp.float32), axis=0)
            pairs = pairs.reshape(groups * CAP, 128)
            total = joined(lax.dot_general(
                picker, pairs, (((0,), (0,)), ((), ())),
                preferred_element_type=jnp.float32, precision=lax.Precision.HIGHEST,
            ))
            column = lax.dot_general(
                pairs, picker, (((0,), (0,)), ((), ())),
                preferred_element_type=jnp.float32, precision=lax.Precision.HIGHEST,
            )
            dens_ref[...] = (column[0:1] + column[64:65]) / clu_rows
        sums = unfold(jnp.sum(zrecv[b][..., :half].astype(jnp.float32), axis=0))
        drift += choose(picks[b], sums)
        if b < last:
            for dz, dc in sources:
                outward(b, lax.rem(z + dz, nz), dc).wait_send()
    drift_ref[...] = drift * ((0.5 * math.sqrt(width)) / total)
    for dz, dc in sources:
        outward(last, lax.rem(z + dz, nz), dc).wait_send()


def shards(candidates, cluster_ids, pool, pool_valid):
    count, width = candidates.shape
    groups = lax.axis_size("clu")
    slabs = lax.axis_size("slab")
    ny = 2 if slabs % 2 == 0 else 1
    nz = slabs // ny
    pool_rows = pool.shape[0]
    tiles = TILES
    peers = groups * slabs
    half = width // 2
    sub = CAP // PARTS
    vmem = pl.BlockSpec(memory_space=pltpu.VMEM)
    hbm = pl.BlockSpec(memory_space=pltpu.HBM)
    dims = (groups, nz, ny, tiles, float(pool_rows * slabs))
    stages = [
        pltpu.VMEM((nz, groups, 2 * sub, half + (128 if b == PARTS - 1 else 0)), jnp.bfloat16)
        for b in range(PARTS)
    ]
    held = pltpu.VMEM((nz, groups, 2 * sub, half), jnp.float32)
    sem = pltpu.SemaphoreType.DMA
    drift, density = pl.pallas_call(
        functools.partial(kernel, dims),
        out_shape=(
            pltpu.VMEM((count, width), jnp.float32),
            pltpu.VMEM((1, count), jnp.float32),
        ),
        in_specs=[hbm, hbm, hbm, hbm],
        out_specs=(vmem, vmem),
        scratch_shapes=[
            pltpu.VMEM((count, width), jnp.bfloat16),
            pltpu.VMEM((1, count), jnp.int32),
            pltpu.VMEM((tiles, 1, pool_rows // tiles), jnp.int32),
            pltpu.VMEM((pool_rows, width), jnp.bfloat16),
            pltpu.VMEM((tiles, width, pool_rows // tiles), jnp.bfloat16),
            pltpu.VMEM((count // sub, 2 * sub, half), jnp.bfloat16),
            pltpu.VMEM((PARTS, ny, nz, groups, 2 * sub, half), jnp.bfloat16),
            pltpu.VMEM((tiles, peers * sub, pool_rows // tiles), jnp.bfloat16),
            *stages,
            *stages,
            *[held] * PARTS,
            *stages,
            *stages,
            sem((3,)),
            sem((tiles,)),
            sem((PARTS * peers,)),
            sem((PARTS * peers,)),
            sem((ny * nz,)),
            sem((ny * nz,)),
            sem((PARTS * nz,)),
            sem((PARTS * nz,)),
            sem((PARTS * nz * groups,)),
            sem((PARTS * nz * groups,)),
        ],
        compiler_params=pltpu.CompilerParams(
            collective_id=0, has_side_effects=True, vmem_limit_bytes=63480000
        ),
    )(
        candidates,
        cluster_ids.reshape(1, count),
        pool_valid.reshape(tiles, 1, pool_rows // tiles),
        pool,
    )
    return (drift, density.reshape(count))


def solution(mesh):
    return jax.shard_map(
        shards,
        mesh=mesh,
        in_specs=(
            P(("grp", "clu", "slab"), None),
            P(("grp", "clu", "slab"), None),
            P(("grp", "clu", "slab"), None),
            P(("grp", "clu", "slab")),
        ),
        out_specs=(P(("grp", "clu", "slab"), None), P(("grp", "clu", "slab"))),
        check_vma=False,
    )
```

```python
import functools
import math

import jax
import jax.numpy as jnp
from jax import lax
from jax.experimental import pallas as pl
from jax.experimental.pallas import tpu as pltpu
from jax.sharding import PartitionSpec as P

CAP = 16
PARTS = 2
TILES = 2
MESH = pl.DeviceIdType.MESH


def rms_rows(data):
    wide = data.astype(jnp.float32)
    factor = lax.rsqrt(jnp.mean(wide * wide, axis=-1, keepdims=True) + 1e-06)
    return (wide * factor).astype(jnp.bfloat16)


def fold(values, sub):
    half = values.shape[1] // 2
    values = values.reshape(-1, sub, 2 * half)
    return jnp.concatenate([values[..., :half], values[..., half:]], axis=1)


def unfold(values):
    blocks, double, half = values.shape
    sub = double // 2
    values = jnp.concatenate([values[:, :sub], values[:, sub:]], axis=2)
    return values.reshape(blocks * sub, 2 * half)


def kernel(dims, cand_hbm, ids_hbm, valid_hbm, pool_hbm, drift_ref, dens_ref,
           cand_ref, ids_ref, valid_ref, unit, turned, outgoing, every, low,
           *rest):
    ysend, yrecv, own, zsend, zrecv = (rest[i * PARTS : (i + 1) * PARTS] for i in range(5))
    in_sem, pool_sem, s1, r1, s2, r2, sy, ry, sz, rz = rest[5 * PARTS :]
    groups, nz, ny, tiles, clu_rows = dims
    count, width = cand_ref.shape
    pool_rows = pool_hbm.shape[0]
    rows_tile = pool_rows // tiles
    sharp = 2.0 * math.sqrt(width)
    sub = CAP // PARTS
    half = width // 2
    c = lax.axis_index("clu")
    slab = lax.axis_index("slab")
    z, y = lax.div(slab, ny), lax.rem(slab, ny)

    def spot(dc, dy, pz):
        return {"clu": lax.rem(c + dc, groups), "slab": pz * ny + lax.rem(y + dy, ny)}

    paired = nz & (nz - 1) == 0

    def partner(dz, back=False):
        if not paired:
            return lax.rem(z + (nz - dz if back else dz), nz)
        place, bit = z, 1
        while bit <= dz:
            if dz & bit:
                place = place + bit - 2 * bit * lax.rem(lax.div(z, bit), 2)
            bit *= 2
        return place

    def device(dc, dy, dz):
        return spot(dc, dy, partner(dz))

    def planned(src, dst, send, i, recv, j, where):
        return pltpu.make_async_remote_copy(
            src_ref=src, dst_ref=dst, send_sem=send.at[i], recv_sem=recv.at[j],
            device_id=where, device_id_type=MESH,
        )

    def remote(src, dst, send, recv, i, where):
        copy = planned(src, dst, send, i, recv, i, where)
        copy.start()
        return copy

    hops = sorted(range(1, nz), key=lambda d: (1 - d % 2, d))
    near = [(dc, 0, dz) for dz in hops for dc in range(groups)]
    side = [(dc, 1, 0) for dc in range(groups)] if ny == 2 else []
    twin = [(dc, 0, 0) for dc in range(1, groups)]
    direct = side + near + twin

    def index(b, offset):
        return ((b * groups + offset[0]) * ny + offset[1]) * nz + offset[2]

    inputs = []
    for i, (src, dst) in enumerate(
        [(cand_hbm, cand_ref), (ids_hbm, ids_ref), (valid_hbm, valid_ref)]
    ):
        load = pltpu.make_async_copy(src, dst, in_sem.at[i])
        load.start()
        inputs.append(load)
    loads = []
    for t in range(tiles):
        span = pl.ds(t * rows_tile, rows_tile)
        load = pltpu.make_async_copy(pool_hbm.at[span], unit.at[span], pool_sem.at[t])
        load.start()
        loads.append(load)

    barrier = pltpu.get_barrier_semaphore()
    for offset in direct:
        pl.semaphore_signal(barrier, inc=1, device_id=device(*offset), device_id_type=MESH)

    inputs[0].wait()
    inputs[1].wait()
    ids = ids_ref[...]
    member = (
        lax.broadcasted_iota(jnp.int32, (groups, count), 0) == ids
    ).astype(jnp.float32)
    upper = (
        lax.broadcasted_iota(jnp.int32, (count, count), 0)
        <= lax.broadcasted_iota(jnp.int32, (count, count), 1)
    ).astype(jnp.float32)
    ranks = jnp.dot(member, upper, preferred_element_type=jnp.float32)
    place = (jnp.sum(member * ranks, axis=0, keepdims=True) - 1.0).astype(jnp.int32)

    def one_hot(rows, slot):
        return lax.broadcasted_iota(jnp.int32, (rows, count), 0) == slot

    lower = jnp.sum(member[0:1], axis=1, keepdims=True).astype(jnp.int32)
    rank = jnp.where(ids == 0, place, place + lower)
    shared = (rank >= sub) & (rank < CAP)
    inner = jnp.where(rank >= CAP, rank - CAP, jnp.where(shared, rank - sub, rank))
    picker = one_hot(
        groups * CAP, ids * CAP + jnp.where(shared, sub, 0) + inner
    ).astype(jnp.float32)
    picks = [
        one_hot(groups * sub, jnp.where(shared == (b == 1), ids * sub + inner, -1))
        for b in range(PARTS)
    ]
    sent = jnp.dot(
        one_hot(count, rank).astype(jnp.bfloat16), rms_rows(cand_ref[...]),
        preferred_element_type=jnp.float32,
    )
    outgoing[...] = fold(sent, sub).astype(jnp.bfloat16)
    every[0, 0, z, c] = outgoing[2 * c]
    every[1, 0, z, c] = outgoing[1]

    pl.semaphore_wait(barrier, len(direct))

    copies, twins = {}, {}

    def spread(b, offset):
        src = outgoing.at[1] if b else outgoing.at[2 * lax.rem(c + offset[0], groups)]
        copies[b, offset] = remote(
            src, every.at[b, offset[1], z, c], s1, r1, index(b, offset), device(*offset)
        )

    def hand_over(dy, dz):
        block = every.at[1, dy, partner(dz, True), c]
        twins[dy, dz] = remote(block, block, s2, r2, dy * nz + dz, spot(1, 0, z))

    for offset in direct:
        spread(0, offset)
    for t in range(tiles):
        loads[t].wait()
        span = pl.ds(t * rows_tile, rows_tile)
        value = rms_rows(unit[span])
        unit[span] = value
        turned[t] = value.T
        if t == 0:
            for offset in direct:
                if offset[0] == 0:
                    spread(1, offset)
            hand_over(0, 0)
    inputs[2].wait()

    for b in range(PARTS):
        for dz in hops:
            for dc in range(groups if b == 0 else 1):
                copies[b, (dc, 0, dz)].wait_recv()
                if ny == 2:
                    fz = partner(dz, True)
                    fc = lax.rem(c + groups - dc, groups)
                    copies[b, (dc, 1, dz)] = remote(
                        every.at[b, 0, fz, fc], every.at[b, 1, fz, fc],
                        s1, r1, index(b, (dc, 1, dz)), device(0, 1, 0),
                    )
                if b == 1:
                    hand_over(0, dz)

    line = nz * groups * sub
    total_rows = ny * line

    def score(b):
        rows = unfold(
            every[b].reshape(ny * nz * groups, 2 * sub, half).astype(jnp.float32)
        ).astype(jnp.bfloat16)
        total = jnp.zeros((total_rows, 1), jnp.float32)
        for t in range(tiles):
            dots = jnp.dot(rows, turned[t], preferred_element_type=jnp.float32)
            weight = valid_ref[t].astype(jnp.float32) * jnp.exp(dots * (sharp / width))
            low[t] = weight.astype(jnp.bfloat16)
            total += jnp.sum(weight, axis=1, keepdims=True)
        return total.reshape(ny, nz * groups, sub, 1)

    def add_up():
        summed = jnp.zeros((total_rows, width), jnp.float32)
        for t in range(tiles):
            summed += jnp.dot(
                low[t], unit[t * rows_tile : (t + 1) * rows_tile],
                preferred_element_type=jnp.float32,
            )
        return fold(summed, sub).reshape(ny, nz, groups, 2 * sub, half)

    def halves(mass):
        high = jnp.broadcast_to(mass, mass.shape[:-1] + (64,)).astype(jnp.bfloat16)
        rest = (mass - high.astype(jnp.float32)).astype(jnp.bfloat16)
        return jnp.concatenate([high, rest], axis=-1)

    def joined(pair):
        return pair[..., 0:1] + pair[..., 64:65]

    me = z * groups + c
    sources = [(dz, dc) for dz in range(nz) for dc in range(groups) if (dz, dc) != (0, 0)]
    turns = sum(([a, nz - 1 - a] for a in range((nz + 1) // 2)), [])[:nz]
    across = {}

    reach = 1
    last = PARTS - 1

    def outward(b, pz, dc):
        pc = lax.rem(c + dc, groups)
        at = b * nz * groups
        return planned(
            zsend[b].at[pz, pc], zrecv[b].at[z, c], sz, at + pz * groups + pc, rz, at + me,
            spot(dc, 0, pz),
        )

    def pass_on(b, pz):
        @pl.when(z != pz)
        def _():
            outward(b, pz, 0).start()

        @pl.when(z == pz)
        def _():
            zrecv[b][z, c] = zsend[b][pz, c]

        for dc in range(1, groups):
            outward(b, pz, dc).start()

    def collect(b):
        for dz, dc in sources:
            pz, pc = lax.rem(z + dz, nz), lax.rem(c + dc, groups)
            block = zrecv[b].at[pz, pc]
            j = (b * nz + pz) * groups + pc
            planned(block, block, sz, j, rz, j, spot(dc, 0, pz)).wait_recv()

    totals = []
    for b in range(PARTS):
        if b == 0:
            for offset in side + twin:
                copies[b, offset].wait_recv()
            if ny == 2:
                for dz in hops:
                    for dc in range(groups):
                        copies[b, (dc, 1, dz)].wait_recv()
        else:
            for copy in twins.values():
                copy.wait_recv()
        totals.append(score(b))
        if b == 0 and ny == 2:
            for dz in [0] + hops:
                copies[1, (0, 1, dz)].wait_recv()
                hand_over(1, dz)
        summed = add_up()
        if b == last:
            mass = jnp.concatenate(totals, axis=2).reshape(ny, nz, groups, CAP, 1)
        if ny == 2:
            for k, pz in enumerate(turns):
                ysend[b][k, :, :, :half] = summed[1, pz].astype(jnp.bfloat16)
                if b == last:
                    ysend[b][k, :, :, half:] = halves(mass[1, pz])
                if (k + 1) % reach == 0 or k == nz - 1:
                    lo = k // reach * reach
                    span = pl.ds(lo, k + 1 - lo)
                    across[b, lo] = remote(
                        ysend[b].at[span], yrecv[b].at[span],
                        sy, ry, b * nz + lo, spot(0, 1, z),
                    )
        own[b][...] = summed[0]

    for b in range(PARTS):
        for k, pz in enumerate(turns):
            value = own[b][pz]
            if ny == 2:
                if k % reach == 0:
                    across[b, k].wait_recv()
                value += yrecv[b][k, :, :, :half].astype(jnp.float32)
            zsend[b][pz, :, :, :half] = value.astype(jnp.bfloat16)
            if b == last:
                value = mass[0, pz]
                if ny == 2:
                    value += joined(yrecv[b][k, :, :, half:].astype(jnp.float32))
                zsend[b][pz, :, :, half:] = halves(value)
            pass_on(b, pz)

    def choose(pick, values):
        pick = pick.astype(jnp.bfloat16)
        high = values.astype(jnp.bfloat16)
        rest = (values - high.astype(jnp.float32)).astype(jnp.bfloat16)
        return sum(
            lax.dot_general(
                pick, x, (((0,), (0,)), ((), ())), preferred_element_type=jnp.float32
            )
            for x in (high, rest)
        )

    for copy in list(copies.values()) + list(twins.values()) + list(across.values()):
        copy.wait_send()
    drift = jnp.zeros((count, width), jnp.float32)
    for b in range(PARTS):
        collect(b)
        if b == last:
            pairs = jnp.sum(zrecv[b][..., half:].astype(jnp.float32), axis=0)
            pairs = pairs.reshape(groups * CAP, 128)
            total = joined(lax.dot_general(
                picker, pairs, (((0,), (0,)), ((), ())),
                preferred_element_type=jnp.float32, precision=lax.Precision.HIGHEST,
            ))
            column = lax.dot_general(
                pairs, picker, (((0,), (0,)), ((), ())),
                preferred_element_type=jnp.float32, precision=lax.Precision.HIGHEST,
            )
            dens_ref[...] = (column[0:1] + column[64:65]) / clu_rows
        sums = unfold(jnp.sum(zrecv[b][..., :half].astype(jnp.float32), axis=0))
        drift += choose(picks[b], sums)
        if b < last:
            for dz, dc in sources:
                outward(b, lax.rem(z + dz, nz), dc).wait_send()
    drift_ref[...] = drift * ((0.5 * math.sqrt(width)) / total)
    for dz, dc in sources:
        outward(last, lax.rem(z + dz, nz), dc).wait_send()


def shards(candidates, cluster_ids, pool, pool_valid):
    count, width = candidates.shape
    groups = lax.axis_size("clu")
    slabs = lax.axis_size("slab")
    ny = 2 if slabs % 2 == 0 else 1
    nz = slabs // ny
    pool_rows = pool.shape[0]
    tiles = TILES
    peers = groups * slabs
    half = width // 2
    sub = CAP // PARTS
    vmem = pl.BlockSpec(memory_space=pltpu.VMEM)
    hbm = pl.BlockSpec(memory_space=pltpu.HBM)
    dims = (groups, nz, ny, tiles, float(pool_rows * slabs))
    stages = [
        pltpu.VMEM((nz, groups, 2 * sub, half + (128 if b == PARTS - 1 else 0)), jnp.bfloat16)
        for b in range(PARTS)
    ]
    held = pltpu.VMEM((nz, groups, 2 * sub, half), jnp.float32)
    sem = pltpu.SemaphoreType.DMA
    drift, density = pl.pallas_call(
        functools.partial(kernel, dims),
        out_shape=(
            pltpu.VMEM((count, width), jnp.float32),
            pltpu.VMEM((1, count), jnp.float32),
        ),
        in_specs=[hbm, hbm, hbm, hbm],
        out_specs=(vmem, vmem),
        scratch_shapes=[
            pltpu.VMEM((count, width), jnp.bfloat16),
            pltpu.VMEM((1, count), jnp.int32),
            pltpu.VMEM((tiles, 1, pool_rows // tiles), jnp.int32),
            pltpu.VMEM((pool_rows, width), jnp.bfloat16),
            pltpu.VMEM((tiles, width, pool_rows // tiles), jnp.bfloat16),
            pltpu.VMEM((count // sub, 2 * sub, half), jnp.bfloat16),
            pltpu.VMEM((PARTS, ny, nz, groups, 2 * sub, half), jnp.bfloat16),
            pltpu.VMEM((tiles, peers * sub, pool_rows // tiles), jnp.bfloat16),
            *stages,
            *stages,
            *[held] * PARTS,
            *stages,
            *stages,
            sem((3,)),
            sem((tiles,)),
            sem((PARTS * peers,)),
            sem((PARTS * peers,)),
            sem((ny * nz,)),
            sem((ny * nz,)),
            sem((PARTS * nz,)),
            sem((PARTS * nz,)),
            sem((PARTS * nz * groups,)),
            sem((PARTS * nz * groups,)),
        ],
        compiler_params=pltpu.CompilerParams(
            collective_id=0, has_side_effects=True, vmem_limit_bytes=63480000
        ),
    )(
        candidates,
        cluster_ids.reshape(1, count),
        pool_valid.reshape(tiles, 1, pool_rows // tiles),
        pool,
    )
    return (drift, density.reshape(count))


def solution(mesh):
    return jax.shard_map(
        shards,
        mesh=mesh,
        in_specs=(
            P(("grp", "clu", "slab"), None),
            P(("grp", "clu", "slab"), None),
            P(("grp", "clu", "slab"), None),
            P(("grp", "clu", "slab")),
        ),
        out_specs=(P(("grp", "clu", "slab"), None), P(("grp", "clu", "slab"))),
        check_vma=False,
    )
```
